32 devices in a mesh: col: 4 (over y, x), tile: 8 (over z, core).
Axes of the slice: x: 2, y: 2, z: 4, core: 2. Of those that a mesh axis runs over, the one named last changes fastest.
Arguments:
- vectors: float32 [8, 4, 64, 2048], P(None, None, 'tile', 'col'), may hold values from -12 to 12
- onsite: float32 [4, 64, 2048], P(None, 'tile', 'col'), may hold values from -0.3 to 0.3
- intra_hop: float32 [3, 2, 64, 2048], P(None, None, 'tile', 'col'), may hold values from 0.15 to 0.35
- inter_index: int32 [4, 2, 64, 2048], P(None, None, 'tile', 'col'), may hold values from 0 to 18
- inter_hop: float32 [4, 2, 64, 2048], P(None, None, 'tile', 'col'), may hold values from 0.04 to 0.16
Outputs:
- last_term: float32 [8, 4, 64, 2048], P(None, None, 'tile', 'col')
- moments: float32 [7, 8], replicated
The draws below stay inside these ranges and needn't reach their ends.
Inputs may be any that keep to these rules, and one draw needn't show every extreme that they name: `inter_index`: A code c below 18 names the second-layer orbital of sublattice c // 9 in the cell at offset ((c % 9) // 3 - 1, c % 3 - 1) from the slot's cell; 18 marks an empty slot.
All inputs are finite; a program needn't handle non-finite values.
Results may differ from the reference program's by a relative error of at most 0.000025.
Values sent between devices are 32-bit elements; how exact they have to be, the bound alone decides.
A program may use at most 64 MiB of HBM per device.

```python
import jax
import jax.numpy as jnp

VECS = 8
K = 4
NA = 64
NB = 2048


def draw_vectors(key, part):
    first_key = jax.random.fold_in(jax.random.fold_in(key, 7), 0)
    positions = jnp.arange(NA, dtype=jnp.float32) / NA
    ramp = jnp.exp(jnp.log(3.0) * positions)[:, None]
    base = jnp.clip(jax.random.normal(first_key, (VECS, 4, NA, NB), jnp.float32), -4.0, 4.0)
    return base * ramp


def touch_ends(values, key, low, largest):
    index_at = [jax.random.randint(jax.random.fold_in(key, axis), (), 0, length) for axis, length in enumerate(values.shape)]
    longest = values.shape.index(max(values.shape))
    neighbour = index_at[:longest] + [(index_at[longest] + 1) % values.shape[longest]] + index_at[longest + 1:]
    return values.at[tuple(index_at)].set(low).at[tuple(neighbour)].set(largest)


def shard_levels(own_key, extent, cuts, least, high):
    def one(axis_at, shards_of):
        draws = jax.random.uniform(jax.random.fold_in(jax.random.fold_in(own_key, 6), axis_at), (shards_of,), jnp.float32, least / len(cuts), high / len(cuts))
        return jnp.repeat(jnp.exp(draws), extent[axis_at] // shards_of).reshape((-1,) + (1,) * (len(extent) - axis_at - 1))

    level = one(*cuts[0])
    for cut in cuts[1:]:
        level = level * one(*cut)
    return level


def setup_inputs(seed: int = 0) -> dict:
    seeds = jax.random.split(jax.random.key(seed), 6)
    vectors = draw_vectors(jax.random.fold_in(seeds[5], 71), 0)
    onsite = jnp.clip(jax.random.uniform(seeds[1], (4, NA, NB), jnp.float32, -0.3, 0.3) * shard_levels(seeds[1], (4, NA, NB), ((1, 8), (2, 4)), -0.4, 0.0), -0.3, 0.3)
    intra_hop = jnp.clip(0.15 + 0.19999999 * jax.random.uniform(seeds[2], (3, 2, NA, NB), jnp.float32) ** shard_levels(seeds[2], (3, 2, NA, NB), ((2, 8), (3, 4)), -0.2, 0.2), 0.15, 0.35)
    inter_index = touch_ends(jax.random.randint(seeds[3], (K, 2, NA, NB), 0, 19), jax.random.fold_in(seeds[3], 1), 0, 18).astype(jnp.int32)
    inter_hop = jnp.clip(0.04 + 0.12 * jax.random.uniform(seeds[4], (K, 2, NA, NB), jnp.float32) ** shard_levels(seeds[4], (K, 2, NA, NB), ((2, 8), (3, 4)), -0.2, 0.2), 0.04, 0.16)
    return {"vectors": vectors, "onsite": onsite, "intra_hop": intra_hop, "inter_index": inter_index, "inter_hop": inter_hop}


BOND_OFFSETS = ((0, 0), (-1, 0), (0, -1))


def rolled(array, row_off, col_off):
    return jnp.roll(array, (-row_off, -col_off), axis=(-2, -1))


def make_weights(neighbours, amplitude):
    return jnp.stack([jnp.sum(jnp.where(neighbours == code_no, amplitude, jnp.zeros_like(amplitude)), axis=0) for code_no in range(18)], axis=1)


def apply_hamiltonian(vector, onsite, intra_hop, weights, pick):
    outputs = []
    for layer_no in range(2):
        side_a = vector[:, 2 * layer_no]
        side_b = vector[:, 2 * layer_no + 1]
        out_a = pick(onsite[2 * layer_no], 0, 0) * pick(side_a, 0, 0)
        out_b = pick(onsite[2 * layer_no + 1], 0, 0) * pick(side_b, 0, 0)
        for bond_idx in range(3):
            row_off, col_off = BOND_OFFSETS[bond_idx]
            out_a = out_a + pick(intra_hop[bond_idx, layer_no], 0, 0) * pick(side_b, row_off, col_off)
            out_b = out_b + pick(intra_hop[bond_idx, layer_no], -row_off, -col_off) * pick(side_a, -row_off, -col_off)
        outputs += [out_a, out_b]
    for source in range(2):
        for code_no in range(18):
            target = code_no // 9
            row_off = (code_no % 9) // 3 - 1
            col_off = code_no % 3 - 1
            outputs[source] = outputs[source] + pick(weights[source, code_no], 0, 0) * pick(vector[:, 2 + target], row_off, col_off)
            outputs[2 + target] = outputs[2 + target] + pick(weights[source, code_no], -row_off, -col_off) * pick(vector[:, source], -row_off, -col_off)
    return jnp.stack(outputs, axis=1)


def inner_sums(left, right):
    return jnp.sum(left * right, axis=(1, 2, 3))


def moments_from(totals, orbitals):
    scaled = totals / orbitals
    zeroth = scaled[0]
    first = scaled[1]
    return jnp.stack([zeroth, first, 2.0 * scaled[2] - zeroth, 2.0 * scaled[3] - first, 2.0 * scaled[4] - zeroth, 2.0 * scaled[5] - first, 2.0 * scaled[6] - zeroth])


def reference(vectors, onsite, intra_hop, inter_index, inter_hop):
    weights = make_weights(inter_index, inter_hop)

    def operator(vector):
        return apply_hamiltonian(vector, onsite, intra_hop, weights, rolled)

    term_zero = vectors
    term_one = operator(term_zero)
    term_two = 2.0 * operator(term_one) - term_zero
    last_term = 2.0 * operator(term_two) - term_one
    totals = jnp.stack([inner_sums(term_zero, term_zero), inner_sums(term_one, term_zero), inner_sums(term_one, term_one), inner_sums(term_two, term_one), inner_sums(term_two, term_two), inner_sums(last_term, term_two), inner_sums(last_term, last_term)])
    return last_term, moments_from(totals, 4 * NA * NB)
```

```python
import functools

import jax
import jax.numpy as jnp
from jax import lax
from jax.experimental import pallas as pl
from jax.experimental.pallas import tpu as pltpu
from jax.sharding import PartitionSpec as P

RIM = 3
LANES = 128
CODES = 18
MESH = pl.DeviceIdType.MESH
BONDS = ((0, 0), (-1, 0), (0, -1))
HOP, CODE, SITE, BOND2 = 4, 5, 6, 7


def kernel(
    n_col, n_tile, orbitals,
    v_ref, onsite_ref, intra_ref, index_ref, hop_ref,
    out_ref, mom_ref,
    area, terms, moved, weights, weights_t, bond_t, packs, halo, sums, part, col_buf, col_sum, tile_buf,
    row_send, row_recv, pack_send, pack_recv, col_send, col_recv, tile_send, tile_recv,
):
    rows = v_ref.shape[2]
    cols = v_ref.shape[3]
    blocks = cols // LANES
    ring = cols + LANES
    my_col = lax.axis_index("col")
    my_tile = lax.axis_index("tile")
    lane = lax.broadcasted_iota(jnp.int32, (8, LANES), 1)
    sub = lax.broadcasted_iota(jnp.int32, (8, LANES), 0)

    def col_at(step):
        return lax.rem(my_col + step + n_col, n_col)

    def tile_at(step):
        return lax.rem(my_tile + step + n_tile, n_tile)

    barrier = pltpu.get_barrier_semaphore()
    greeted = [(col_at(c), tile_at(t)) for c in (-1, 1) for t in (-1, 1)]
    greeted += [(col_at(c), my_tile) for c in range(1, n_col)]
    for c, t in greeted:
        pl.semaphore_signal(barrier, inc=1, device_id=(c, t), device_id_type=MESH)

    def greet(i, carry):
        pl.semaphore_signal(barrier, inc=1, device_id=(my_col, lax.rem(my_tile + i, n_tile)), device_id_type=MESH)
        return carry

    lax.fori_loop(1, n_tile, greet, 0)

    own = slice(RIM, RIM + rows)
    for o in range(4):
        area[o, own, :, 0:cols] = jnp.swapaxes(v_ref[:, o], 0, 1)
    area[HOP, own, :, 0:cols] = jnp.swapaxes(hop_ref[...], 0, 1)
    area[CODE, own, :, 0:cols] = jnp.swapaxes(index_ref[...].astype(jnp.float32), 0, 1)
    area[SITE, own, :, 0:cols] = jnp.swapaxes(
        jnp.concatenate([onsite_ref[...], intra_ref[0:4]], axis=0), 0, 1
    )
    area[BOND2, own, :, 0:cols] = jnp.swapaxes(
        jnp.concatenate([intra_ref[4:6], jnp.zeros((6, rows, cols), jnp.float32)], axis=0), 0, 1
    )

    pl.semaphore_wait(barrier, len(greeted) + n_tile - 1)

    row_copies = []
    for way, (src, dst, step) in enumerate(((rows, 0, 1), (RIM, RIM + rows, -1))):
        copy = pltpu.make_async_remote_copy(
            src_ref=area.at[:, src : src + RIM, :, 0:cols],
            dst_ref=area.at[:, dst : dst + RIM, :, 0:cols],
            send_sem=row_send.at[way],
            recv_sem=row_recv.at[way],
            device_id=(my_col, tile_at(step)),
            device_id_type=MESH,
        )
        copy.start()
        row_copies.append(copy)

    def pack(r, carry):
        out = list(carry)
        for g in range(8):
            i = (g % 4) * rows + r
            hit = lane // 4 == i
            left = pltpu.roll(area[g, RIM + r, :, 0:LANES], 4 * i, 1)
            right = pltpu.roll(area[g, RIM + r, :, cols - LANES : cols], lax.rem(4 * i + 4, LANES), 1)
            out[g // 4] = jnp.where(hit, left, out[g // 4])
            out[2 + g // 4] = jnp.where(hit, right, out[2 + g // 4])
        return tuple(out)

    zero = jnp.zeros((8, LANES), jnp.float32)
    packed = lax.fori_loop(0, rows, pack, (zero,) * 4)
    for n in range(4):
        packs[n // 2, n % 2] = packed[n]

    pack_copies = []
    for side, step in ((0, -1), (1, 1)):
        for dt in (0, -1, 1):
            slot = side * 3 + 1 - dt
            copy = pltpu.make_async_remote_copy(
                src_ref=packs.at[side],
                dst_ref=halo.at[slot],
                send_sem=pack_send.at[slot],
                recv_sem=pack_recv.at[slot],
                device_id=(col_at(step), tile_at(dt)),
                device_id_type=MESH,
            )
            copy.start()
            pack_copies.append(copy)

    wide = lax.broadcasted_iota(jnp.int32, (8, ring), 0)

    def rolls(x):
        return pltpu.roll(x, 1, 1), pltpu.roll(x, ring - 1, 1)

    def prepare(r, theirs, dt):
        for g in range(8):
            i = (g % 4) * rows + theirs
            from_right = pltpu.roll(halo[1 + dt, g // 4], lax.rem(LANES - 4 * i, LANES), 1)
            from_left = pltpu.roll(halo[4 + dt, g // 4], LANES - 4 - 4 * i, 1)
            area[g, r, :, cols:ring] = jnp.where(lane < LANES // 2, from_right, from_left)
        for o in range(4):
            moved[0, 0, o, r], moved[0, 1, o, r] = rolls(area[o, r])
        bond_t[r] = rolls(area[BOND2, r])[1]
        for s in range(2):
            for b in range(blocks + 1):
                at = slice(b * LANES, (b + 1) * LANES)
                total = [zero] * 3
                for k in range(4):
                    f = 2 * k + s
                    code = jnp.broadcast_to(area[CODE, r, f : f + 1, at], (8, LANES)).astype(jnp.int32)
                    hop = jnp.broadcast_to(area[HOP, r, f : f + 1, at], (8, LANES))
                    for g in range(3):
                        total[g] = total[g] + jnp.where(code == sub + 8 * g, hop, 0.0)
                for g in range(3):
                    weights[r, s, 8 * g : 8 * g + 8, at] = total[g]
            for g in range(3):
                x = weights[r, s, 8 * g : 8 * g + 8, :]
                back, ahead = rolls(x)
                rest = lax.rem(wide + 8 * g, 3)
                weights_t[r, s, 8 * g : 8 * g + 8, :] = jnp.where(
                    rest == 0, ahead, jnp.where(rest == 2, back, x)
                )

    def term(k, o, r, at):
        return area[o, r, :, at] if k == 0 else terms[k - 1, o, r, :, at]

    def hamiltonian(k, r, at):
        def v(o, row_off, col_off):
            if col_off == 0:
                return term(k, o, r + row_off, at)
            return moved[k, (col_off + 1) // 2, o, r + row_off, :, at]

        def spread(x):
            return jnp.broadcast_to(x, (8, LANES))

        def site(f, row):
            return spread(area[SITE, row, f : f + 1, at])

        outs = []
        for l in range(2):
            a, b = 2 * l, 2 * l + 1
            f0, f1 = site(4 + l, r), site(6 + l, r)
            f2 = spread(area[BOND2, r, l : l + 1, at])
            outs.append(
                site(a, r) * v(a, 0, 0) + f0 * v(b, 0, 0) + f1 * v(b, -1, 0) + f2 * v(b, 0, -1)
            )
            outs.append(
                site(b, r) * v(b, 0, 0)
                + f0 * v(a, 0, 0)
                + site(6 + l, r + 1) * v(a, 1, 0)
                + spread(bond_t[r, l : l + 1, at]) * v(a, 0, 1)
            )
        for s in range(2):
            for c in range(CODES):
                t, e, f = c // 9, c % 9 // 3 - 1, c % 3 - 1
                outs[s] = outs[s] + spread(weights[r, s, c : c + 1, at]) * v(2 + t, e, f)
                outs[2 + t] = outs[2 + t] + spread(weights_t[r - e, s, c : c + 1, at]) * v(s, -e, -f)
        return outs

    def advance(k, r):
        inside = jnp.where((r >= RIM) & (r < RIM + rows), 1.0, 0.0).astype(jnp.float32)
        cross, square, first = zero, zero, zero
        for b in range(blocks + 1 if k < 2 else blocks):
            at = slice(b * LANES, (b + 1) * LANES)
            outs = hamiltonian(k, r, at)
            for o in range(4):
                old = term(k, o, r, at)
                new = outs[o] if k == 0 else 2.0 * outs[o] - term(k - 1, o, r, at)
                terms[k, o, r, :, at] = new
                if b < blocks:
                    cross = cross + new * old
                    square = square + new * new
                    if k == 0:
                        first = first + old * old
        if k == 0:
            sums[0] += inside * first
        sums[2 * k + 1] += inside * cross
        sums[2 * k + 2] += inside * square
        if k < 2:
            for o in range(4):
                moved[k + 1, 0, o, r], moved[k + 1, 1, o, r] = rolls(terms[k, o, r])

    def loop(low, high, body):
        def step(i, carry):
            body(i)
            return carry

        lax.fori_loop(low, high, step, 0)

    for n in range(7):
        sums[n] = zero

    for n in (0, 3):
        pack_copies[n].wait_recv()
    loop(RIM, RIM + rows, lambda r: prepare(r, r - RIM, 0))
    for k in range(3):
        loop(RIM + 1 + k, RIM + rows - 1 - k, functools.partial(advance, k))

    for n in (1, 2, 4, 5):
        pack_copies[n].wait_recv()
    for copy in row_copies:
        copy.wait_recv()
    loop(0, RIM, lambda r: prepare(r, rows - RIM + r, -1))
    loop(0, RIM, lambda r: prepare(RIM + rows + r, r, 1))
    for k in range(3):
        def outer(i, k=k):
            advance(k, k + 1 + i + (i // 3) * (rows - 2 * k - 2))

        loop(0, 6, outer)

    row = jnp.zeros((8, LANES), jnp.float32)
    for n in range(7):
        total = jnp.sum(sums[n], axis=1, keepdims=True)
        row = jnp.where(lane == sub + 8 * n, jnp.broadcast_to(total, (8, LANES)), row)
    part[...] = jnp.sum(row, axis=0, keepdims=True)
    col_buf[my_col] = part[...]
    col_copies = []
    for step in range(1, n_col):
        copy = pltpu.make_async_remote_copy(
            src_ref=part,
            dst_ref=col_buf.at[my_col],
            send_sem=col_send.at[step],
            recv_sem=col_recv.at[step],
            device_id=(col_at(step), my_tile),
            device_id_type=MESH,
        )
        copy.start()
        col_copies.append(copy)
    for o in range(4):
        out_ref[:, o] = jnp.swapaxes(terms[2, o, own, :, 0:cols], 0, 1)

    def col_done(step):
        return pltpu.make_async_remote_copy(
            src_ref=part,
            dst_ref=col_buf.at[col_at(-step)],
            send_sem=col_send.at[step],
            recv_sem=col_recv.at[step],
            device_id=(col_at(step), my_tile),
            device_id_type=MESH,
        )

    for step in range(1, n_col):
        col_done(step).wait_recv()
    total = col_buf[0]
    for n in range(1, n_col):
        total = total + col_buf[n]
    col_sum[...] = total
    tile_buf[my_tile] = col_sum[...]

    def tile_copy(step, slot):
        return pltpu.make_async_remote_copy(
            src_ref=col_sum,
            dst_ref=tile_buf.at[slot],
            send_sem=tile_send.at[step],
            recv_sem=tile_recv.at[step],
            device_id=(my_col, lax.rem(my_tile + step, n_tile)),
            device_id_type=MESH,
        )

    loop(1, n_tile, lambda i: tile_copy(i, my_tile).start())
    for copy in row_copies + pack_copies + col_copies:
        copy.wait_send()
    loop(1, n_tile, lambda i: tile_copy(i, lax.rem(my_tile + n_tile - i, n_tile)).wait_recv())
    loop(1, n_tile, lambda i: tile_copy(i, my_tile).wait_send())
    total = lax.fori_loop(1, n_tile, lambda i, t: t + tile_buf[i], tile_buf[0])
    total = jnp.broadcast_to(total / orbitals, (8, LANES))
    scaled = [pltpu.roll(total, (LANES - 8 * n) % LANES, 1)[0:1, 0:8] for n in range(7)]
    mom_ref[0:1, :] = scaled[0]
    mom_ref[1:2, :] = scaled[1]
    for n in range(2, 7):
        mom_ref[n : n + 1, :] = 2.0 * scaled[n] - scaled[n % 2]


def on_device(n_col, n_tile, vectors, onsite, intra_hop, inter_index, inter_hop):
    count, _, rows, cols = vectors.shape
    slots = inter_index.shape[0]
    assert count == 8 and slots == 4 and rows == 8 and cols % LANES == 0
    tall = rows + 2 * RIM
    ring = cols + LANES
    f32 = jnp.float32
    vmem = pl.BlockSpec(memory_space=pltpu.VMEM)
    dma = pltpu.SemaphoreType.DMA
    return pl.pallas_call(
        functools.partial(kernel, n_col, n_tile, 4 * rows * cols * n_col * n_tile),
        out_shape=(
            jax.ShapeDtypeStruct(vectors.shape, f32),
            jax.ShapeDtypeStruct((7, count), f32),
        ),
        in_specs=[vmem] * 5,
        out_specs=(vmem, vmem),
        scratch_shapes=[
            pltpu.VMEM((8, tall, 8, ring), f32),
            pltpu.VMEM((3, 4, tall, 8, ring), f32),
            pltpu.VMEM((3, 2, 4, tall, 8, ring), f32),
            pltpu.VMEM((tall, 2, 24, ring), f32),
            pltpu.VMEM((tall, 2, 24, ring), f32),
            pltpu.VMEM((tall, 8, ring), f32),
            pltpu.VMEM((2, 2, 8, LANES), f32),
            pltpu.VMEM((6, 2, 8, LANES), f32),
            pltpu.VMEM((7, 8, LANES), f32),
            pltpu.VMEM((1, LANES), f32),
            pltpu.VMEM((n_col, 1, LANES), f32),
            pltpu.VMEM((1, LANES), f32),
            pltpu.VMEM((n_tile, 1, LANES), f32),
            dma((2,)), dma((2,)), dma((6,)), dma((6,)),
            dma((n_col,)), dma((n_col,)), dma((n_tile,)), dma((n_tile,)),
        ],
        compiler_params=pltpu.CompilerParams(
            collective_id=0, has_side_effects=True, vmem_limit_bytes=48 << 20
        ),
    )(
        vectors,
        onsite,
        intra_hop.reshape(6, rows, cols),
        inter_index.reshape(2 * slots, rows, cols),
        inter_hop.reshape(2 * slots, rows, cols),
    )


def solution(mesh):
    spec4, spec3 = P(None, None, "tile", "col"), P(None, "tile", "col")
    return jax.shard_map(
        functools.partial(on_device, mesh.shape["col"], mesh.shape["tile"]),
        mesh=mesh,
        in_specs=(spec4, spec3, spec4, spec4, spec4),
        out_specs=(spec4, P()),
        check_vma=False,
    )
```

```python
import functools

import jax
import jax.numpy as jnp
from jax import lax
from jax.experimental import pallas as pl
from jax.experimental.pallas import tpu as pltpu
from jax.sharding import PartitionSpec as P

RIM = 2
LANES = 128
CODES = 18
MESH = pl.DeviceIdType.MESH
BONDS = ((0, 0), (-1, 0), (0, -1))
HOP, CODE, SITE, BOND2 = 4, 5, 6, 7


def kernel(
    n_col, n_tile, orbitals,
    v_hbm, onsite_hbm, intra_hbm, index_hbm, hop_hbm,
    out_ref, mom_ref,
    v_ref, onsite_ref, intra_ref, index_ref, hop_ref, load_sem,
    area, terms, moved, weights, weights_t, bond_t, packs, halo, sums, part, col_buf, col_sum, tile_buf,
    row_send, row_recv, pack_send, pack_recv, col_send, col_recv, tile_send, tile_recv,
):
    rows = v_ref.shape[2]
    cols = v_ref.shape[3]
    blocks = cols // LANES
    ring = cols + LANES
    my_col = lax.axis_index("col")
    my_tile = lax.axis_index("tile")
    lane = lax.broadcasted_iota(jnp.int32, (8, LANES), 1)
    sub = lax.broadcasted_iota(jnp.int32, (8, LANES), 0)

    def col_at(step):
        return lax.rem(my_col + step + n_col, n_col)

    def tile_at(step):
        return lax.rem(my_tile + step + n_tile, n_tile)

    loads = [
        pltpu.make_async_copy(src, dst, load_sem.at[n])
        for n, (src, dst) in enumerate(
            (
                (v_hbm, v_ref),
                (hop_hbm, hop_ref),
                (index_hbm, index_ref),
                (onsite_hbm, onsite_ref),
                (intra_hbm, intra_ref),
            )
        )
    ]
    for load in loads:
        load.start()

    barrier = pltpu.get_barrier_semaphore()
    greeted = [(col_at(c), tile_at(t)) for c in (-1, 1) for t in (-1, 1)]
    greeted += [(col_at(c), my_tile) for c in range(1, n_col)]
    for c, t in greeted:
        pl.semaphore_signal(barrier, inc=1, device_id=(c, t), device_id_type=MESH)

    def greet(i, carry):
        pl.semaphore_signal(barrier, inc=1, device_id=(my_col, lax.rem(my_tile + i, n_tile)), device_id_type=MESH)
        return carry

    lax.fori_loop(1, n_tile, greet, 0)

    for load in loads:
        load.wait()
    own = slice(RIM, RIM + rows)
    for o in range(4):
        area[o, own, :, 0:cols] = jnp.swapaxes(v_ref[:, o], 0, 1)
    area[HOP, own, :, 0:cols] = jnp.swapaxes(hop_ref[...], 0, 1)
    area[CODE, own, :, 0:cols] = jnp.swapaxes(index_ref[...].astype(jnp.float32), 0, 1)
    area[SITE, own, :, 0:cols] = jnp.swapaxes(
        jnp.concatenate([onsite_ref[...], intra_ref[0:4]], axis=0), 0, 1
    )
    area[BOND2, own, :, 0:cols] = jnp.swapaxes(
        jnp.concatenate([intra_ref[4:6], jnp.zeros((6, rows, cols), jnp.float32)], axis=0), 0, 1
    )

    pl.semaphore_wait(barrier, len(greeted) + n_tile - 1)

    rim_copies = []

    def send_rim(layer, way, src, dst):
        copy = pltpu.make_async_remote_copy(
            src_ref=src,
            dst_ref=dst,
            send_sem=row_send.at[layer, way],
            recv_sem=row_recv.at[layer, way],
            device_id=(my_col, tile_at(1 - 2 * way)),
            device_id_type=MESH,
        )
        copy.start()
        rim_copies.append(copy)

    low, high = RIM, RIM + rows
    for layer in range(2):
        for way in range(2):
            src, dst = ((high - 1 - layer, low - 1 - layer), (low + layer, high + layer))[way]
            groups = 8 if layer == 0 else 6 + way
            send_rim(
                layer, way,
                area.at[0:groups, src : src + 1, :, 0:cols],
                area.at[0:groups, dst : dst + 1, :, 0:cols],
            )

    def pack(r, carry):
        out = list(carry)
        for g in range(8):
            i = (g % 4) * rows + r
            hit = lane // 4 == i
            left = pltpu.roll(area[g, RIM + r, :, 0:LANES], 4 * i, 1)
            right = pltpu.roll(area[g, RIM + r, :, cols - LANES : cols], lax.rem(4 * i + 4, LANES), 1)
            out[g // 4] = jnp.where(hit, left, out[g // 4])
            out[2 + g // 4] = jnp.where(hit, right, out[2 + g // 4])
        return tuple(out)

    zero = jnp.zeros((8, LANES), jnp.float32)
    packed = lax.fori_loop(0, rows, pack, (zero,) * 4)
    for n in range(4):
        packs[n // 2, n % 2] = packed[n]

    pack_copies = []
    for side, step in ((0, -1), (1, 1)):
        for dt in (0, -1, 1):
            slot = side * 3 + 1 - dt
            copy = pltpu.make_async_remote_copy(
                src_ref=packs.at[side],
                dst_ref=halo.at[slot],
                send_sem=pack_send.at[slot],
                recv_sem=pack_recv.at[slot],
                device_id=(col_at(step), tile_at(dt)),
                device_id_type=MESH,
            )
            copy.start()
            pack_copies.append(copy)

    wide = lax.broadcasted_iota(jnp.int32, (8, ring), 0)

    def rolls(x):
        return pltpu.roll(x, 1, 1), pltpu.roll(x, ring - 1, 1)

    def prepare(r, theirs, dt, groups=8):
        for g in range(groups):
            i = (g % 4) * rows + theirs
            from_right = pltpu.roll(halo[1 + dt, g // 4], lax.rem(LANES - 4 * i, LANES), 1)
            from_left = pltpu.roll(halo[4 + dt, g // 4], LANES - 4 - 4 * i, 1)
            area[g, r, :, cols:ring] = jnp.where(lane < LANES // 2, from_right, from_left)
        for o in range(4):
            moved[0, 0, o, r], moved[0, 1, o, r] = rolls(area[o, r])
        if groups == 8:
            bond_t[r] = rolls(area[BOND2, r])[1]
        for s in range(2):
            for b in range(blocks + 1):
                at = slice(b * LANES, (b + 1) * LANES)
                total = [zero] * 3
                for k in range(4):
                    f = 2 * k + s
                    code = jnp.broadcast_to(area[CODE, r, f : f + 1, at], (8, LANES)).astype(jnp.int32)
                    hop = jnp.broadcast_to(area[HOP, r, f : f + 1, at], (8, LANES))
                    for g in range(3):
                        total[g] = total[g] + jnp.where(code == sub + 8 * g, hop, 0.0)
                for g in range(3):
                    weights[r, s, 8 * g : 8 * g + 8, at] = total[g]
            for g in range(3):
                x = weights[r, s, 8 * g : 8 * g + 8, :]
                back, ahead = rolls(x)
                rest = lax.rem(wide + 8 * g, 3)
                weights_t[r, s, 8 * g : 8 * g + 8, :] = jnp.where(
                    rest == 0, ahead, jnp.where(rest == 2, back, x)
                )

    def term(k, o, r, at):
        return area[o, r, :, at] if k == 0 else terms[k - 1, o, r, :, at]

    def hamiltonian(k, r, at):
        def v(o, row_off, col_off):
            if col_off == 0:
                return term(k, o, r + row_off, at)
            return moved[k, (col_off + 1) // 2, o, r + row_off, :, at]

        def spread(x):
            return jnp.broadcast_to(x, (8, LANES))

        def site(f, row):
            return spread(area[SITE, row, f : f + 1, at])

        outs = []
        for l in range(2):
            a, b = 2 * l, 2 * l + 1
            f0, f1 = site(4 + l, r), site(6 + l, r)
            f2 = spread(area[BOND2, r, l : l + 1, at])
            outs.append(
                site(a, r) * v(a, 0, 0) + f0 * v(b, 0, 0) + f1 * v(b, -1, 0) + f2 * v(b, 0, -1)
            )
            outs.append(
                site(b, r) * v(b, 0, 0)
                + f0 * v(a, 0, 0)
                + site(6 + l, r + 1) * v(a, 1, 0)
                + spread(bond_t[r, l : l + 1, at]) * v(a, 0, 1)
            )
        for s in range(2):
            for c in range(CODES):
                t, e, f = c // 9, c % 9 // 3 - 1, c % 3 - 1
                outs[s] = outs[s] + spread(weights[r, s, c : c + 1, at]) * v(2 + t, e, f)
                outs[2 + t] = outs[2 + t] + spread(weights_t[r - e, s, c : c + 1, at]) * v(s, -e, -f)
        return outs

    def advance(k, r):
        inside = jnp.where((r >= RIM) & (r < RIM + rows), 1.0, 0.0).astype(jnp.float32)
        cross, square, first = zero, zero, zero
        for b in range(blocks + 1 if k < 2 else blocks):
            at = slice(b * LANES, (b + 1) * LANES)
            outs = hamiltonian(k, r, at)
            for o in range(4):
                old = term(k, o, r, at)
                new = outs[o] if k == 0 else 2.0 * outs[o] - term(k - 1, o, r, at)
                terms[k, o, r, :, at] = new
                if b < blocks:
                    cross = cross + new * old
                    square = square + new * new
                    if k == 0:
                        first = first + old * old
        if k == 0:
            sums[0] += inside * first
        sums[2 * k + 1] += inside * cross
        sums[2 * k + 2] += inside * square
        if k < 2:
            for o in range(4):
                moved[k + 1, 0, o, r], moved[k + 1, 1, o, r] = rolls(terms[k, o, r])

    def loop(low, high, body):
        def step(i, carry):
            body(i)
            return carry

        lax.fori_loop(low, high, step, 0)

    for n in range(7):
        sums[n] = zero

    for n in (0, 3):
        pack_copies[n].wait_recv()
    loop(low, high, lambda r: prepare(r, r - low, 0))
    for k in range(3):
        loop(low + 1 + k, high - 1 - k, functools.partial(advance, k))
        if k == 1:
            send_rim(2, 0, terms.at[0, :, high - 2 : high - 1], terms.at[0, :, 0:1])
            send_rim(2, 1, terms.at[0, :, low + 1 : low + 2], terms.at[0, :, high + 1 : high + 2])

    for n in (1, 2, 4, 5):
        pack_copies[n].wait_recv()
    for layer in range(3):
        for way in range(2):
            rim_copies[2 * layer + way].wait_recv()
        if layer < 2:
            prepare(low - 1 - layer, rows - 1 - layer, -1, 8 if layer == 0 else 6)
            prepare(high + layer, layer, 1, 8 if layer == 0 else 7)
        else:
            for r in (0, high + 1):
                for o in range(4):
                    moved[1, 0, o, r], moved[1, 1, o, r] = rolls(terms[0, o, r])
        for k in range(1 if layer == 2 else 0, 3):
            top, bottom = low - layer + k, high - 1 + layer - k
            loop(0, 2, lambda i, k=k: advance(k, top + i * (bottom - top)))

    row = jnp.zeros((8, LANES), jnp.float32)
    for n in range(7):
        total = jnp.sum(sums[n], axis=1, keepdims=True)
        row = jnp.where(lane == sub + 8 * n, jnp.broadcast_to(total, (8, LANES)), row)
    part[...] = jnp.sum(row, axis=0, keepdims=True)
    col_buf[my_col] = part[...]
    col_copies = []
    for step in range(1, n_col):
        copy = pltpu.make_async_remote_copy(
            src_ref=part,
            dst_ref=col_buf.at[my_col],
            send_sem=col_send.at[step],
            recv_sem=col_recv.at[step],
            device_id=(col_at(step), my_tile),
            device_id_type=MESH,
        )
        copy.start()
        col_copies.append(copy)
    for o in range(4):
        out_ref[:, o] = jnp.swapaxes(terms[2, o, own, :, 0:cols], 0, 1)

    def col_done(step):
        return pltpu.make_async_remote_copy(
            src_ref=part,
            dst_ref=col_buf.at[col_at(-step)],
            send_sem=col_send.at[step],
            recv_sem=col_recv.at[step],
            device_id=(col_at(step), my_tile),
            device_id_type=MESH,
        )

    for step in range(1, n_col):
        col_done(step).wait_recv()
    total = col_buf[0]
    for n in range(1, n_col):
        total = total + col_buf[n]
    col_sum[...] = total
    tile_buf[my_tile] = col_sum[...]

    def tile_copy(step, slot):
        return pltpu.make_async_remote_copy(
            src_ref=col_sum,
            dst_ref=tile_buf.at[slot],
            send_sem=tile_send.at[step],
            recv_sem=tile_recv.at[step],
            device_id=(my_col, lax.rem(my_tile + step, n_tile)),
            device_id_type=MESH,
        )

    loop(1, n_tile, lambda i: tile_copy(i, my_tile).start())
    for copy in rim_copies + pack_copies + col_copies:
        copy.wait_send()
    loop(1, n_tile, lambda i: tile_copy(i, lax.rem(my_tile + n_tile - i, n_tile)).wait_recv())
    loop(1, n_tile, lambda i: tile_copy(i, my_tile).wait_send())
    total = lax.fori_loop(1, n_tile, lambda i, t: t + tile_buf[i], tile_buf[0])
    total = jnp.broadcast_to(total / orbitals, (8, LANES))
    scaled = [pltpu.roll(total, (LANES - 8 * n) % LANES, 1)[0:1, 0:8] for n in range(7)]
    mom_ref[0:1, :] = scaled[0]
    mom_ref[1:2, :] = scaled[1]
    for n in range(2, 7):
        mom_ref[n : n + 1, :] = 2.0 * scaled[n] - scaled[n % 2]


def on_device(n_col, n_tile, vectors, onsite, intra_hop, inter_index, inter_hop):
    count, _, rows, cols = vectors.shape
    slots = inter_index.shape[0]
    assert count == 8 and slots == 4 and rows == 8 and cols % LANES == 0
    tall = rows + 2 * RIM
    ring = cols + LANES
    f32 = jnp.float32
    vmem = pl.BlockSpec(memory_space=pltpu.VMEM)
    dma = pltpu.SemaphoreType.DMA
    return pl.pallas_call(
        functools.partial(kernel, n_col, n_tile, 4 * rows * cols * n_col * n_tile),
        out_shape=(
            jax.ShapeDtypeStruct(vectors.shape, f32),
            jax.ShapeDtypeStruct((7, count), f32),
        ),
        in_specs=[pl.BlockSpec(memory_space=pl.ANY)] * 5,
        out_specs=(vmem, vmem),
        scratch_shapes=[
            pltpu.VMEM(vectors.shape, f32),
            pltpu.VMEM(onsite.shape, f32),
            pltpu.VMEM((6, rows, cols), f32),
            pltpu.VMEM((2 * slots, rows, cols), jnp.int32),
            pltpu.VMEM((2 * slots, rows, cols), f32),
            dma((5,)),
            pltpu.VMEM((8, tall, 8, ring), f32),
            pltpu.VMEM((3, 4, tall, 8, ring), f32),
            pltpu.VMEM((3, 2, 4, tall, 8, ring), f32),
            pltpu.VMEM((tall, 2, 24, ring), f32),
            pltpu.VMEM((tall, 2, 24, ring), f32),
            pltpu.VMEM((tall, 8, ring), f32),
            pltpu.VMEM((2, 2, 8, LANES), f32),
            pltpu.VMEM((6, 2, 8, LANES), f32),
            pltpu.VMEM((7, 8, LANES), f32),
            pltpu.VMEM((1, LANES), f32),
            pltpu.VMEM((n_col, 1, LANES), f32),
            pltpu.VMEM((1, LANES), f32),
            pltpu.VMEM((n_tile, 1, LANES), f32),
            dma((3, 2)), dma((3, 2)), dma((6,)), dma((6,)),
            dma((n_col,)), dma((n_col,)), dma((n_tile,)), dma((n_tile,)),
        ],
        compiler_params=pltpu.CompilerParams(
            collective_id=0, has_side_effects=True, vmem_limit_bytes=60 << 20
        ),
    )(
        vectors,
        onsite,
        intra_hop.reshape(6, rows, cols),
        inter_index.reshape(2 * slots, rows, cols),
        inter_hop.reshape(2 * slots, rows, cols),
    )


def solution(mesh):
    spec4, spec3 = P(None, None, "tile", "col"), P(None, "tile", "col")
    return jax.shard_map(
        functools.partial(on_device, mesh.shape["col"], mesh.shape["tile"]),
        mesh=mesh,
        in_specs=(spec4, spec3, spec4, spec4, spec4),
        out_specs=(spec4, P()),
        check_vma=False,
    )
```

```python
import functools

import jax
import jax.numpy as jnp
from jax import lax
from jax.experimental import pallas as pl
from jax.experimental.pallas import tpu as pltpu
from jax.sharding import PartitionSpec as P

RIM = 2
LANES = 128
CODES = 18
MESH = pl.DeviceIdType.MESH
BONDS = ((0, 0), (-1, 0), (0, -1))
HOP, CODE, SITE, BOND2 = 4, 5, 6, 7


def kernel(
    n_col, n_tile, orbitals,
    v_hbm, onsite_hbm, intra_hbm, index_hbm, hop_hbm,
    out_ref, mom_ref,
    v_ref, onsite_ref, intra_ref, index_ref, hop_ref, load_sem,
    area, terms, moved, weights, weights_t, bond_t, packs, halo, sums, part, all_parts,
    row_send, row_recv, pack_send, pack_recv, part_send, part_recv,
):
    rows = v_ref.shape[2]
    cols = v_ref.shape[3]
    blocks = cols // LANES
    ring = cols + LANES
    my_col = lax.axis_index("col")
    my_tile = lax.axis_index("tile")
    lane = lax.broadcasted_iota(jnp.int32, (8, LANES), 1)
    sub = lax.broadcasted_iota(jnp.int32, (8, LANES), 0)

    def col_at(step):
        return lax.rem(my_col + step + n_col, n_col)

    def tile_at(step):
        return lax.rem(my_tile + step + n_tile, n_tile)

    loads = [
        pltpu.make_async_copy(src, dst, load_sem.at[n])
        for n, (src, dst) in enumerate(
            (
                (v_hbm, v_ref),
                (hop_hbm, hop_ref),
                (index_hbm, index_ref),
                (onsite_hbm, onsite_ref),
                (intra_hbm, intra_ref),
            )
        )
    ]
    for load in loads:
        load.start()

    barrier = pltpu.get_barrier_semaphore()
    devices = n_col * n_tile
    me = my_col * n_tile + my_tile

    def device(step):
        at = lax.rem(me + step, devices)
        return (lax.div(at, n_tile), lax.rem(at, n_tile))

    def greet(i, carry):
        pl.semaphore_signal(barrier, inc=1, device_id=device(i), device_id_type=MESH)
        return carry

    lax.fori_loop(1, devices, greet, 0)

    for load in loads:
        load.wait()
    own = slice(RIM, RIM + rows)
    for o in range(4):
        area[o, own, :, 0:cols] = jnp.swapaxes(v_ref[:, o], 0, 1)
    area[HOP, own, :, 0:cols] = jnp.swapaxes(hop_ref[...], 0, 1)
    area[CODE, own, :, 0:cols] = jnp.swapaxes(index_ref[...].astype(jnp.float32), 0, 1)
    area[SITE, own, :, 0:cols] = jnp.swapaxes(
        jnp.concatenate([onsite_ref[...], intra_ref[0:4]], axis=0), 0, 1
    )
    area[BOND2, own, :, 0:cols] = jnp.swapaxes(
        jnp.concatenate([intra_ref[4:6], jnp.zeros((6, rows, cols), jnp.float32)], axis=0), 0, 1
    )

    def pack(r, carry):
        out = list(carry)
        for g in range(8):
            i = (g % 4) * rows + r
            hit = lane // 4 == i
            left = pltpu.roll(area[g, RIM + r, :, 0:LANES], 4 * i, 1)
            right = pltpu.roll(area[g, RIM + r, :, cols - LANES : cols], lax.rem(4 * i + 4, LANES), 1)
            out[g // 4] = jnp.where(hit, left, out[g // 4])
            out[2 + g // 4] = jnp.where(hit, right, out[2 + g // 4])
        return tuple(out)

    zero = jnp.zeros((8, LANES), jnp.float32)
    packed = lax.fori_loop(0, rows, pack, (zero,) * 4)
    for n in range(4):
        packs[n // 2, n % 2] = packed[n]

    def weigh(r, at_blocks):
        for s in range(2):
            for b in at_blocks:
                at = slice(b * LANES, (b + 1) * LANES)
                total = [zero] * 3
                for k in range(4):
                    f = 2 * k + s
                    code = jnp.broadcast_to(area[CODE, r, f : f + 1, at], (8, LANES)).astype(jnp.int32)
                    hop = jnp.broadcast_to(area[HOP, r, f : f + 1, at], (8, LANES))
                    for g in range(3):
                        total[g] = total[g] + jnp.where(code == sub + 8 * g, hop, 0.0)
                for g in range(3):
                    weights[r, s, 8 * g : 8 * g + 8, at] = total[g]

    def loop(low, high, body):
        def step(i, carry):
            body(i)
            return carry

        lax.fori_loop(low, high, step, 0)

    low, high = RIM, RIM + rows
    loop(low, high, lambda r: weigh(r, range(blocks)))
    for n in range(7):
        sums[n] = zero

    pl.semaphore_wait(barrier, devices - 1)

    pack_copies = []
    for side, step in ((0, -1), (1, 1)):
        for dt in (0, -1, 1):
            slot = side * 3 + 1 - dt
            copy = pltpu.make_async_remote_copy(
                src_ref=packs.at[side],
                dst_ref=halo.at[slot],
                send_sem=pack_send.at[slot],
                recv_sem=pack_recv.at[slot],
                device_id=(col_at(step), tile_at(dt)),
                device_id_type=MESH,
            )
            copy.start()
            pack_copies.append(copy)


    rim_copies = []

    def send_rim(layer, way, src, dst):
        copy = pltpu.make_async_remote_copy(
            src_ref=src,
            dst_ref=dst,
            send_sem=row_send.at[layer, way],
            recv_sem=row_recv.at[layer, way],
            device_id=(my_col, tile_at(1 - 2 * way)),
            device_id_type=MESH,
        )
        copy.start()
        rim_copies.append(copy)

    for layer in range(2):
        for way in range(2):
            src, dst = ((high - 1 - layer, low - 1 - layer), (low + layer, high + layer))[way]
            groups = 8 if layer == 0 else 6 + way
            send_rim(
                layer, way,
                area.at[0:groups, src : src + 1, :, 0:cols],
                area.at[0:groups, dst : dst + 1, :, 0:cols],
            )

    wide = lax.broadcasted_iota(jnp.int32, (8, ring), 0)

    def rolls(x):
        return pltpu.roll(x, 1, 1), pltpu.roll(x, ring - 1, 1)

    def prepare(r, theirs, dt, groups=8):
        for g in range(groups):
            i = (g % 4) * rows + theirs
            from_right = pltpu.roll(halo[1 + dt, g // 4], lax.rem(LANES - 4 * i, LANES), 1)
            from_left = pltpu.roll(halo[4 + dt, g // 4], LANES - 4 - 4 * i, 1)
            area[g, r, :, cols:ring] = jnp.where(lane < LANES // 2, from_right, from_left)
        for o in range(4):
            moved[0, 0, o, r], moved[0, 1, o, r] = rolls(area[o, r])
        if groups == 8:
            bond_t[r] = rolls(area[BOND2, r])[1]
        weigh(r, (blocks,) if dt == 0 else range(blocks + 1))
        for s in range(2):
            for g in range(3):
                x = weights[r, s, 8 * g : 8 * g + 8, :]
                back, ahead = rolls(x)
                rest = lax.rem(wide + 8 * g, 3)
                weights_t[r, s, 8 * g : 8 * g + 8, :] = jnp.where(
                    rest == 0, ahead, jnp.where(rest == 2, back, x)
                )

    def term(k, o, r, at):
        return area[o, r, :, at] if k == 0 else terms[k - 1, o, r, :, at]

    def hamiltonian(k, r, at):
        def v(o, row_off, col_off):
            if col_off == 0:
                return term(k, o, r + row_off, at)
            return moved[k, (col_off + 1) // 2, o, r + row_off, :, at]

        def spread(x):
            return jnp.broadcast_to(x, (8, LANES))

        def site(f, row):
            return spread(area[SITE, row, f : f + 1, at])

        outs = []
        for l in range(2):
            a, b = 2 * l, 2 * l + 1
            f0, f1 = site(4 + l, r), site(6 + l, r)
            f2 = spread(area[BOND2, r, l : l + 1, at])
            outs.append(
                site(a, r) * v(a, 0, 0) + f0 * v(b, 0, 0) + f1 * v(b, -1, 0) + f2 * v(b, 0, -1)
            )
            outs.append(
                site(b, r) * v(b, 0, 0)
                + f0 * v(a, 0, 0)
                + site(6 + l, r + 1) * v(a, 1, 0)
                + spread(bond_t[r, l : l + 1, at]) * v(a, 0, 1)
            )
        for s in range(2):
            for c in range(CODES):
                t, e, f = c // 9, c % 9 // 3 - 1, c % 3 - 1
                outs[s] = outs[s] + spread(weights[r, s, c : c + 1, at]) * v(2 + t, e, f)
                outs[2 + t] = outs[2 + t] + spread(weights_t[r - e, s, c : c + 1, at]) * v(s, -e, -f)
        return outs

    def advance(k, r):
        inside = jnp.where((r >= RIM) & (r < RIM + rows), 1.0, 0.0).astype(jnp.float32)
        cross, square, first = zero, zero, zero
        for b in range(blocks + 1 if k < 2 else blocks):
            at = slice(b * LANES, (b + 1) * LANES)
            outs = hamiltonian(k, r, at)
            for o in range(4):
                old = term(k, o, r, at)
                new = outs[o] if k == 0 else 2.0 * outs[o] - term(k - 1, o, r, at)
                terms[k, o, r, :, at] = new
                if b < blocks:
                    cross = cross + new * old
                    square = square + new * new
                    if k == 0:
                        first = first + old * old
        if k == 0:
            sums[0] += inside * first
        sums[2 * k + 1] += inside * cross
        sums[2 * k + 2] += inside * square
        if k < 2:
            for o in range(4):
                moved[k + 1, 0, o, r], moved[k + 1, 1, o, r] = rolls(terms[k, o, r])

    for n in (0, 3):
        pack_copies[n].wait_recv()
    loop(low, high, lambda r: prepare(r, r - low, 0))
    for k in range(3):
        loop(low + 1 + k, high - 1 - k, functools.partial(advance, k))
        if k == 1:
            send_rim(2, 0, terms.at[0, :, high - 2 : high - 1], terms.at[0, :, 0:1])
            send_rim(2, 1, terms.at[0, :, low + 1 : low + 2], terms.at[0, :, high + 1 : high + 2])

    for n in (1, 2, 4, 5):
        pack_copies[n].wait_recv()
    for layer in range(3):
        for way in range(2):
            rim_copies[2 * layer + way].wait_recv()
        if layer < 2:
            prepare(low - 1 - layer, rows - 1 - layer, -1, 8 if layer == 0 else 6)
            prepare(high + layer, layer, 1, 8 if layer == 0 else 7)
        else:
            for r in (0, high + 1):
                for o in range(4):
                    moved[1, 0, o, r], moved[1, 1, o, r] = rolls(terms[0, o, r])
        for k in range(1 if layer == 2 else 0, 3):
            top, bottom = low - layer + k, high - 1 + layer - k
            loop(0, 2, lambda i, k=k: advance(k, top + i * (bottom - top)))

    row = jnp.zeros((8, LANES), jnp.float32)
    for n in range(7):
        total = jnp.sum(sums[n], axis=1, keepdims=True)
        row = jnp.where(lane == sub + 8 * n, jnp.broadcast_to(total, (8, LANES)), row)
    part[...] = jnp.sum(row, axis=0, keepdims=True)
    all_parts[me] = part[...]

    def part_copy(step, slot):
        return pltpu.make_async_remote_copy(
            src_ref=part,
            dst_ref=all_parts.at[slot],
            send_sem=part_send.at[step],
            recv_sem=part_recv.at[step],
            device_id=device(step),
            device_id_type=MESH,
        )

    loop(1, devices, lambda i: part_copy(i, me).start())
    for o in range(4):
        out_ref[:, o] = jnp.swapaxes(terms[2, o, own, :, 0:cols], 0, 1)

    for copy in rim_copies + pack_copies:
        copy.wait_send()
    loop(1, devices, lambda i: part_copy(i, lax.rem(me + devices - i, devices)).wait_recv())
    loop(1, devices, lambda i: part_copy(i, me).wait_send())
    total = all_parts[0]
    for n in range(1, devices):
        total = total + all_parts[n]
    total = jnp.broadcast_to(total / orbitals, (8, LANES))
    scaled = [pltpu.roll(total, (LANES - 8 * n) % LANES, 1)[0:1, 0:8] for n in range(7)]
    mom_ref[0:1, :] = scaled[0]
    mom_ref[1:2, :] = scaled[1]
    for n in range(2, 7):
        mom_ref[n : n + 1, :] = 2.0 * scaled[n] - scaled[n % 2]


def on_device(n_col, n_tile, vectors, onsite, intra_hop, inter_index, inter_hop):
    count, _, rows, cols = vectors.shape
    slots = inter_index.shape[0]
    assert count == 8 and slots == 4 and rows == 8 and cols % LANES == 0
    tall = rows + 2 * RIM
    ring = cols + LANES
    f32 = jnp.float32
    vmem = pl.BlockSpec(memory_space=pltpu.VMEM)
    dma = pltpu.SemaphoreType.DMA
    return pl.pallas_call(
        functools.partial(kernel, n_col, n_tile, 4 * rows * cols * n_col * n_tile),
        out_shape=(
            jax.ShapeDtypeStruct(vectors.shape, f32),
            jax.ShapeDtypeStruct((7, count), f32),
        ),
        in_specs=[pl.BlockSpec(memory_space=pltpu.HBM)] * 5,
        out_specs=(vmem, vmem),
        scratch_shapes=[
            pltpu.VMEM(vectors.shape, f32),
            pltpu.VMEM(onsite.shape, f32),
            pltpu.VMEM((6, rows, cols), f32),
            pltpu.VMEM((2 * slots, rows, cols), jnp.int32),
            pltpu.VMEM((2 * slots, rows, cols), f32),
            dma((5,)),
            pltpu.VMEM((8, tall, 8, ring), f32),
            pltpu.VMEM((3, 4, tall, 8, ring), f32),
            pltpu.VMEM((3, 2, 4, tall, 8, ring), f32),
            pltpu.VMEM((tall, 2, 24, ring), f32),
            pltpu.VMEM((tall, 2, 24, ring), f32),
            pltpu.VMEM((tall, 8, ring), f32),
            pltpu.VMEM((2, 2, 8, LANES), f32),
            pltpu.VMEM((6, 2, 8, LANES), f32),
            pltpu.VMEM((7, 8, LANES), f32),
            pltpu.VMEM((1, LANES), f32),
            pltpu.VMEM((n_col * n_tile, 1, LANES), f32),
            dma((3, 2)), dma((3, 2)), dma((6,)), dma((6,)),
            dma((n_col * n_tile,)), dma((n_col * n_tile,)),
        ],
        compiler_params=pltpu.CompilerParams(
            collective_id=0, has_side_effects=True, vmem_limit_bytes=32 << 20
        ),
    )(
        *(
            pltpu.with_memory_space_constraint(x, pltpu.HBM)
            for x in (
                vectors,
                onsite,
                intra_hop.reshape(6, rows, cols),
                inter_index.reshape(2 * slots, rows, cols),
                inter_hop.reshape(2 * slots, rows, cols),
            )
        )
    )


def solution(mesh):
    spec4, spec3 = P(None, None, "tile", "col"), P(None, "tile", "col")
    return jax.shard_map(
        functools.partial(on_device, mesh.shape["col"], mesh.shape["tile"]),
        mesh=mesh,
        in_specs=(spec4, spec3, spec4, spec4, spec4),
        out_specs=(spec4, P()),
        check_vma=False,
    )
```

```python
import functools

import jax
import jax.numpy as jnp
from jax import lax
from jax.experimental import pallas as pl
from jax.experimental.pallas import tpu as pltpu
from jax.sharding import PartitionSpec as P

RIM = 2
LANES = 128
CODES = 18
MESH = pl.DeviceIdType.MESH
BONDS = ((0, 0), (-1, 0), (0, -1))
HOP, CODE, SITE, BOND2 = 4, 5, 6, 7


def kernel(
    n_col, n_tile, orbitals,
    v_hbm, onsite_hbm, intra_hbm, index_hbm, hop_hbm,
    out_ref, mom_ref,
    v_ref, onsite_ref, intra_ref, index_ref, hop_ref, load_sem,
    area, terms, moved, weights, weights_t, bond_t, packs, halo, sums, part, all_parts,
    row_send, row_recv, pack_send, pack_recv, part_send, part_recv,
):
    rows = v_ref.shape[2]
    cols = v_ref.shape[3]
    blocks = cols // LANES
    ring = cols + LANES
    my_col = lax.axis_index("col")
    my_tile = lax.axis_index("tile")
    lane = lax.broadcasted_iota(jnp.int32, (8, LANES), 1)
    sub = lax.broadcasted_iota(jnp.int32, (8, LANES), 0)

    def col_at(step):
        return lax.rem(my_col + step + n_col, n_col)

    def tile_at(step):
        return lax.rem(my_tile + step + n_tile, n_tile)

    loads = [
        pltpu.make_async_copy(src, dst, load_sem.at[n])
        for n, (src, dst) in enumerate(
            (
                (v_hbm, v_ref),
                (hop_hbm, hop_ref),
                (index_hbm, index_ref),
                (onsite_hbm, onsite_ref),
                (intra_hbm, intra_ref),
            )
        )
    ]
    for load in loads:
        load.start()

    barrier = pltpu.get_barrier_semaphore()
    devices = n_col * n_tile
    me = my_col * n_tile + my_tile

    def device(step):
        at = lax.rem(me + step, devices)
        return (lax.div(at, n_tile), lax.rem(at, n_tile))

    def greet(i, carry):
        pl.semaphore_signal(barrier, inc=1, device_id=device(i), device_id_type=MESH)
        return carry

    lax.fori_loop(1, devices, greet, 0)

    for load in loads:
        load.wait()
    own = slice(RIM, RIM + rows)
    for o in range(4):
        area[o, own, :, 0:cols] = jnp.swapaxes(v_ref[:, o], 0, 1)
    area[HOP, own, :, 0:cols] = jnp.swapaxes(hop_ref[...], 0, 1)
    area[CODE, own, :, 0:cols] = jnp.swapaxes(index_ref[...].astype(jnp.float32), 0, 1)
    area[SITE, own, :, 0:cols] = jnp.swapaxes(
        jnp.concatenate([onsite_ref[...], intra_ref[0:4]], axis=0), 0, 1
    )
    area[BOND2, own, :, 0:cols] = jnp.swapaxes(
        jnp.concatenate([intra_ref[4:6], jnp.zeros((6, rows, cols), jnp.float32)], axis=0), 0, 1
    )

    def pack(r, carry):
        out = list(carry)
        for g in range(8):
            i = (g % 4) * rows + r
            hit = lane // 4 == i
            left = pltpu.roll(area[g, RIM + r, :, 0:LANES], 4 * i, 1)
            right = pltpu.roll(area[g, RIM + r, :, cols - LANES : cols], lax.rem(4 * i + 4, LANES), 1)
            out[g // 4] = jnp.where(hit, left, out[g // 4])
            out[2 + g // 4] = jnp.where(hit, right, out[2 + g // 4])
        return tuple(out)

    zero = jnp.zeros((8, LANES), jnp.float32)
    packed = lax.fori_loop(0, rows, pack, (zero,) * 4)
    for n in range(4):
        packs[n // 2, n % 2] = packed[n]

    def weigh(r, at_blocks):
        for s in range(2):
            for b in at_blocks:
                at = slice(b * LANES, (b + 1) * LANES)
                total = [zero] * 3
                for k in range(4):
                    f = 2 * k + s
                    code = jnp.broadcast_to(area[CODE, r, f : f + 1, at], (8, LANES)).astype(jnp.int32)
                    hop = jnp.broadcast_to(area[HOP, r, f : f + 1, at], (8, LANES))
                    for g in range(3):
                        total[g] = total[g] + jnp.where(code == sub + 8 * g, hop, 0.0)
                for g in range(3):
                    weights[r, s, 8 * g : 8 * g + 8, at] = total[g]

    def loop(low, high, body):
        def step(i, carry):
            body(i)
            return carry

        lax.fori_loop(low, high, step, 0)

    low, high = RIM, RIM + rows
    loop(low, high, lambda r: weigh(r, range(blocks)))
    for n in range(7):
        sums[n] = zero

    pl.semaphore_wait(barrier, devices - 1)

    pack_copies = []
    for side, step in ((0, -1), (1, 1)):
        for dt in (0, -1, 1):
            slot = side * 3 + 1 - dt
            copy = pltpu.make_async_remote_copy(
                src_ref=packs.at[side],
                dst_ref=halo.at[slot],
                send_sem=pack_send.at[slot],
                recv_sem=pack_recv.at[slot],
                device_id=(col_at(step), tile_at(dt)),
                device_id_type=MESH,
            )
            copy.start()
            pack_copies.append(copy)


    rim_copies = []

    def send_rim(layer, way, src, dst):
        copy = pltpu.make_async_remote_copy(
            src_ref=src,
            dst_ref=dst,
            send_sem=row_send.at[layer, way],
            recv_sem=row_recv.at[layer, way],
            device_id=(my_col, tile_at(1 - 2 * way)),
            device_id_type=MESH,
        )
        copy.start()
        rim_copies.append(copy)

    for layer in range(2):
        for way in range(2):
            src, dst = ((high - 1 - layer, low - 1 - layer), (low + layer, high + layer))[way]
            groups = 8 if layer == 0 else 6 + way
            send_rim(
                layer, way,
                area.at[0:groups, src : src + 1, :, 0:cols],
                area.at[0:groups, dst : dst + 1, :, 0:cols],
            )

    wide = lax.broadcasted_iota(jnp.int32, (8, ring), 0)

    def rolls(x):
        return pltpu.roll(x, 1, 1), pltpu.roll(x, ring - 1, 1)

    def prepare(r, theirs, dt, groups=8):
        for g in range(groups):
            i = (g % 4) * rows + theirs
            from_right = pltpu.roll(halo[1 + dt, g // 4], lax.rem(LANES - 4 * i, LANES), 1)
            from_left = pltpu.roll(halo[4 + dt, g // 4], LANES - 4 - 4 * i, 1)
            area[g, r, :, cols:ring] = jnp.where(lane < LANES // 2, from_right, from_left)
        for o in range(4):
            moved[0, 0, o, r], moved[0, 1, o, r] = rolls(area[o, r])
        if groups == 8:
            bond_t[r] = rolls(area[BOND2, r])[1]
        weigh(r, (blocks,) if dt == 0 else range(blocks + 1))
        for s in range(2):
            for g in range(3):
                x = weights[r, s, 8 * g : 8 * g + 8, :]
                back, ahead = rolls(x)
                rest = lax.rem(wide + 8 * g, 3)
                weights_t[r, s, 8 * g : 8 * g + 8, :] = jnp.where(
                    rest == 0, ahead, jnp.where(rest == 2, back, x)
                )

    def term(k, o, r, at):
        return area[o, r, :, at] if k == 0 else terms[k - 1, o, r, :, at]

    def hamiltonian(k, r, at):
        def v(o, row_off, col_off):
            if col_off == 0:
                return term(k, o, r + row_off, at)
            return moved[k, (col_off + 1) // 2, o, r + row_off, :, at]

        def spread(x):
            return jnp.broadcast_to(x, (8, LANES))

        def site(f, row):
            return spread(area[SITE, row, f : f + 1, at])

        outs = []
        for l in range(2):
            a, b = 2 * l, 2 * l + 1
            f0, f1 = site(4 + l, r), site(6 + l, r)
            f2 = spread(area[BOND2, r, l : l + 1, at])
            outs.append(
                site(a, r) * v(a, 0, 0) + f0 * v(b, 0, 0) + f1 * v(b, -1, 0) + f2 * v(b, 0, -1)
            )
            outs.append(
                site(b, r) * v(b, 0, 0)
                + f0 * v(a, 0, 0)
                + site(6 + l, r + 1) * v(a, 1, 0)
                + spread(bond_t[r, l : l + 1, at]) * v(a, 0, 1)
            )
        for s in range(2):
            for c in range(CODES):
                t, e, f = c // 9, c % 9 // 3 - 1, c % 3 - 1
                outs[s] = outs[s] + spread(weights[r, s, c : c + 1, at]) * v(2 + t, e, f)
                outs[2 + t] = outs[2 + t] + spread(weights_t[r - e, s, c : c + 1, at]) * v(s, -e, -f)
        return outs

    def advance(k, r):
        inside = jnp.where((r >= RIM) & (r < RIM + rows), 1.0, 0.0).astype(jnp.float32)
        cross, square, first = zero, zero, zero
        for b in range(blocks + 1 if k < 2 else blocks):
            at = slice(b * LANES, (b + 1) * LANES)
            outs = hamiltonian(k, r, at)
            for o in range(4):
                old = term(k, o, r, at)
                new = outs[o] if k == 0 else 2.0 * outs[o] - term(k - 1, o, r, at)
                terms[k, o, r, :, at] = new
                if b < blocks:
                    cross = cross + new * old
                    square = square + new * new
                    if k == 0:
                        first = first + old * old
        if k == 0:
            sums[0] += inside * first
        sums[2 * k + 1] += inside * cross
        sums[2 * k + 2] += inside * square
        if k < 2:
            for o in range(4):
                moved[k + 1, 0, o, r], moved[k + 1, 1, o, r] = rolls(terms[k, o, r])

    for n in (0, 3):
        pack_copies[n].wait_recv()
    loop(low, high, lambda r: prepare(r, r - low, 0))
    for k in range(3):
        loop(low + 1 + k, high - 1 - k, functools.partial(advance, k))
        if k == 1:
            send_rim(2, 0, terms.at[0, :, high - 2 : high - 1], terms.at[0, :, 0:1])
            send_rim(2, 1, terms.at[0, :, low + 1 : low + 2], terms.at[0, :, high + 1 : high + 2])

    for n in (1, 2, 4, 5):
        pack_copies[n].wait_recv()
    for layer in range(3):
        for way in range(2):
            rim_copies[2 * layer + way].wait_recv()
        if layer < 2:
            prepare(low - 1 - layer, rows - 1 - layer, -1, 8 if layer == 0 else 6)
            prepare(high + layer, layer, 1, 8 if layer == 0 else 7)
        else:
            for r in (0, high + 1):
                for o in range(4):
                    moved[1, 0, o, r], moved[1, 1, o, r] = rolls(terms[0, o, r])
        for k in range(1 if layer == 2 else 0, 3):
            top, bottom = low - layer + k, high - 1 + layer - k
            loop(0, 2, lambda i, k=k: advance(k, top + i * (bottom - top)))

    row = jnp.zeros((8, LANES), jnp.float32)
    for n in range(7):
        total = jnp.sum(sums[n], axis=1, keepdims=True)
        row = jnp.where(lane == sub + 8 * n, jnp.broadcast_to(total, (8, LANES)), row)
    part[...] = jnp.sum(row, axis=0, keepdims=True)
    all_parts[me] = part[...]

    def part_copy(step, slot):
        return pltpu.make_async_remote_copy(
            src_ref=part,
            dst_ref=all_parts.at[slot],
            send_sem=part_send.at[step],
            recv_sem=part_recv.at[step],
            device_id=device(step),
            device_id_type=MESH,
        )

    loop(1, devices, lambda i: part_copy(i, me).start())
    for o in range(4):
        out_ref[:, o] = jnp.swapaxes(terms[2, o, own, :, 0:cols], 0, 1)

    for copy in rim_copies + pack_copies:
        copy.wait_send()
    loop(1, devices, lambda i: part_copy(i, lax.rem(me + devices - i, devices)).wait_recv())
    loop(1, devices, lambda i: part_copy(i, me).wait_send())
    total = all_parts[0]
    for n in range(1, devices):
        total = total + all_parts[n]
    total = jnp.broadcast_to(total / orbitals, (8, LANES))
    scaled = [pltpu.roll(total, (LANES - 8 * n) % LANES, 1)[0:1, 0:8] for n in range(7)]
    mom_ref[0:1, :] = scaled[0]
    mom_ref[1:2, :] = scaled[1]
    for n in range(2, 7):
        mom_ref[n : n + 1, :] = 2.0 * scaled[n] - scaled[n % 2]


def emit(last_ref, rows_ref, out_ref, mom_ref, sem):
    copies = [
        pltpu.make_async_copy(last_ref, out_ref, sem.at[0]),
        pltpu.make_async_copy(rows_ref, mom_ref, sem.at[1]),
    ]
    for copy in copies:
        copy.start()
    for copy in copies:
        copy.wait()


def on_device(n_col, n_tile, vectors, onsite, intra_hop, inter_index, inter_hop):
    count, _, rows, cols = vectors.shape
    slots = inter_index.shape[0]
    assert count == 8 and slots == 4 and rows == 8 and cols % LANES == 0
    tall = rows + 2 * RIM
    ring = cols + LANES
    f32 = jnp.float32
    vmem = pl.BlockSpec(memory_space=pltpu.VMEM)
    dma = pltpu.SemaphoreType.DMA
    results = pl.pallas_call(
        functools.partial(kernel, n_col, n_tile, 4 * rows * cols * n_col * n_tile),
        out_shape=(
            jax.ShapeDtypeStruct(vectors.shape, f32),
            jax.ShapeDtypeStruct((7, count), f32),
        ),
        in_specs=[pl.BlockSpec(memory_space=pltpu.HBM)] * 5,
        out_specs=(vmem, vmem),
        scratch_shapes=[
            pltpu.VMEM(vectors.shape, f32),
            pltpu.VMEM(onsite.shape, f32),
            pltpu.VMEM((6, rows, cols), f32),
            pltpu.VMEM((2 * slots, rows, cols), jnp.int32),
            pltpu.VMEM((2 * slots, rows, cols), f32),
            dma((5,)),
            pltpu.VMEM((8, tall, 8, ring), f32),
            pltpu.VMEM((3, 4, tall, 8, ring), f32),
            pltpu.VMEM((3, 2, 4, tall, 8, ring), f32),
            pltpu.VMEM((tall, 2, 24, ring), f32),
            pltpu.VMEM((tall, 2, 24, ring), f32),
            pltpu.VMEM((tall, 8, ring), f32),
            pltpu.VMEM((2, 2, 8, LANES), f32),
            pltpu.VMEM((6, 2, 8, LANES), f32),
            pltpu.VMEM((7, 8, LANES), f32),
            pltpu.VMEM((1, LANES), f32),
            pltpu.VMEM((n_col * n_tile, 1, LANES), f32),
            dma((3, 2)), dma((3, 2)), dma((6,)), dma((6,)),
            dma((n_col * n_tile,)), dma((n_col * n_tile,)),
        ],
        compiler_params=pltpu.CompilerParams(
            collective_id=0, has_side_effects=True, vmem_limit_bytes=32 << 20
        ),
    )(
        *(
            pltpu.with_memory_space_constraint(x, pltpu.HBM)
            for x in (
                vectors,
                onsite,
                intra_hop.reshape(6, rows, cols),
                inter_index.reshape(2 * slots, rows, cols),
                inter_hop.reshape(2 * slots, rows, cols),
            )
        )
    )
    kept = pl.BlockSpec(memory_space=pl.ANY)
    return pl.pallas_call(
        emit,
        out_shape=(
            jax.ShapeDtypeStruct(vectors.shape, f32),
            jax.ShapeDtypeStruct((7, count), f32),
        ),
        in_specs=[kept] * 2,
        out_specs=(kept, kept),
        scratch_shapes=[dma((2,))],
        compiler_params=pltpu.CompilerParams(vmem_limit_bytes=1 << 20),
    )(*results)


def solution(mesh):
    spec4, spec3 = P(None, None, "tile", "col"), P(None, "tile", "col")
    return jax.shard_map(
        functools.partial(on_device, mesh.shape["col"], mesh.shape["tile"]),
        mesh=mesh,
        in_specs=(spec4, spec3, spec4, spec4, spec4),
        out_specs=(spec4, P()),
        check_vma=False,
    )
```
